32 devices in a mesh: row: 8 (over z, y), col: 4 (over x, core).
Axes of the slice: x: 2, y: 2, z: 4, core: 2. Of those that a mesh axis runs over, the one named last changes fastest.
Arguments:
- queries: bfloat16 [12288, 4096], P(('row', 'col')), may hold values from -6 to 6
- keys: bfloat16 [16384, 256], P(('row', 'col')), may hold values from -6 to 6
- values: bfloat16 [16384, 256], P(('row', 'col')), may hold values from -6 to 6
- output_gradient: bfloat16 [12288, 4096], P(('row', 'col')), may hold values from -6 to 6
- tile_block_table: int32 [96, 3], P(('row', 'col')), may hold values from 0 to 31, as said below
Outputs:
- dqueries: bfloat16 [12288, 4096], P(('row', 'col'))
- dkeys: bfloat16 [16384, 256], P(('row', 'col'))
- dvalues: bfloat16 [16384, 256], P(('row', 'col'))
The draws below stay inside these ranges and needn't reach their ends.
Inputs may be any that keep to these rules, and one draw needn't show every extreme that they name: `tile_block_table`: A tile's first id is the block that holds its own query rows; its 3 ids are distinct and none is larger than that block. Block b is held by the device of index b // 1 in the order row-major over (row, col). The tiles of one device name at most 1 distinct blocks held on devices of one col index, and at most 2 distinct blocks held on devices of one row index.
All inputs are finite; a program needn't handle non-finite values.
Results may differ from the reference program's by a relative error of at most 0.0064.
Values may be sent and summed in bfloat16 or wider, within the bound.
No kernel may reach another device: no remote copies, remote signals or barrier semaphores. Data moves between devices by JAX's collectives and lax.ppermute only.
A program may use at most 192 MiB of HBM per device.

```python
import jax
import jax.numpy as jnp
from jax import lax

QUERY_HEADS = 32
KEY_VALUE_HEADS = 2
HEAD_WIDTH = 128
GROUP_WIDTH = 16
TILE_QUERY_ROWS = 128
BLOCK_KEY_ROWS = 512
PICKED_BLOCKS = 3
BLK_DEV = 1
DEVICE_TILES = 3
CAP_COL = 1
CAP_ROW = 2
BLOCK_COUNT = 32
CONTEXT_LENGTH = 16384
TILES = 96
QROWS = 12288
N_ROW = 8
N_COL = 4


def draw_queries(key, part):
    gaussian_portion = jax.random.normal(jax.random.fold_in(key, 21), (QROWS, QUERY_HEADS, HEAD_WIDTH), jnp.float32)
    drawn_blocks = jnp.clip(gaussian_portion, -4.0, 4.0)
    return drawn_blocks.reshape(QROWS, QUERY_HEADS * HEAD_WIDTH).astype(jnp.bfloat16)


def draw_keys(key, part):
    gaussian_portion = jax.random.normal(jax.random.fold_in(key, 31), (CONTEXT_LENGTH, KEY_VALUE_HEADS, HEAD_WIDTH), jnp.float32)
    drawn_blocks = jnp.clip(gaussian_portion, -4.0, 4.0)
    return drawn_blocks.reshape(CONTEXT_LENGTH, KEY_VALUE_HEADS * HEAD_WIDTH).astype(jnp.bfloat16)


def device_lists(device_key, device):
    catalog = jnp.arange(BLOCK_COUNT, dtype=jnp.int32)
    holder = catalog // BLK_DEV
    holder_row = holder // N_COL
    holder_col = holder % N_COL
    same_row = (holder_row[None, :] == holder_row[:, None]).astype(jnp.int32)
    same_col = (holder_col[None, :] == holder_col[:, None]).astype(jnp.int32)
    tile_ids = device * DEVICE_TILES + jnp.arange(DEVICE_TILES, dtype=jnp.int32)
    own_blocks = (BLOCK_COUNT // 4 + tile_ids * TILE_QUERY_ROWS // BLOCK_KEY_ROWS).astype(jnp.int32)
    claimed = (catalog[None, :] == own_blocks[:, None]).astype(jnp.int32)
    chosen = jnp.max(claimed, axis=0)
    picked_ids = [own_blocks]
    for round_index in range(PICKED_BLOCKS - 1):
        column_picks = []
        for tile_index in range(DEVICE_TILES):
            round_key = jax.random.fold_in(device_key, round_index * DEVICE_TILES + tile_index)
            jitter = jax.random.randint(round_key, (BLOCK_COUNT,), 0, 4096)
            own_block = own_blocks[tile_index]
            reward = 2048 * (catalog == 0) + 1536 * (catalog == own_block - 1) + 1024 * (catalog == own_block - 2) + 1024 * chosen
            row_load = jnp.dot(same_row, chosen)
            col_load = jnp.dot(same_col, chosen)
            usable = (catalog < own_block) & (claimed[tile_index] == 0) & ((chosen == 1) | (row_load < CAP_ROW) & (col_load < CAP_COL))
            rating = jnp.where(usable, (reward + jitter) * BLOCK_COUNT + catalog, -1)
            picked = jnp.argmax(rating).astype(jnp.int32)
            marked = (catalog == picked).astype(jnp.int32)
            claimed = claimed.at[tile_index].set(jnp.maximum(claimed[tile_index], marked))
            chosen = jnp.maximum(chosen, marked)
            column_picks.append(picked)
        picked_ids.append(jnp.stack(column_picks))
    return jnp.stack(picked_ids, axis=1)


def draw_tile_block_table(key, part):
    device_keys = jax.random.split(key, N_ROW * N_COL)
    every_list = jax.vmap(device_lists)(device_keys, jnp.arange(N_ROW * N_COL, dtype=jnp.int32))
    return every_list.reshape(TILES, PICKED_BLOCKS).astype(jnp.int32)


def level_of(key, extent, pieces, low, largest):
    def one(axis_at, parts):
        draws = jax.random.uniform(jax.random.fold_in(jax.random.fold_in(key, 6), axis_at), (parts,), jnp.float32, low / len(pieces), largest / len(pieces))
        return jnp.repeat(jnp.exp(draws), extent[axis_at] // parts).reshape((-1,) + (1,) * (len(extent) - axis_at - 1))

    level = one(*pieces[0])
    for cut in pieces[1:]:
        level = level * one(*cut)
    return level


def normal_values(rng, dims, spread, most, shards=(), kind=jnp.bfloat16):
    result = jax.random.normal(rng, dims, jnp.float32) * spread
    if len(shards) > 0:
        result = level_of(rng, dims, shards, -0.22, 0.18) * result
    return jnp.clip(result, min=-most, max=most).astype(kind)


def setup_inputs(seed: int = 0) -> dict:
    key_of = jax.random.split(jax.random.key(seed), 6)
    return {
        "queries": draw_queries(jax.random.fold_in(key_of[5], 71), 0),
        "keys": draw_keys(jax.random.fold_in(key_of[5], 71), 0),
        "values": normal_values(key_of[2], (CONTEXT_LENGTH, KEY_VALUE_HEADS * HEAD_WIDTH), 1.0, 6.0, ((0, 32),)),
        "output_gradient": normal_values(key_of[3], (QROWS, QUERY_HEADS * HEAD_WIDTH), 1.0, 6.0, ((0, 32),)),
        "tile_block_table": draw_tile_block_table(jax.random.fold_in(key_of[5], 71), 0),
    }


def pair_grads(tile_query_rows, gradient_rows, block_key_rows, block_value_rows, query_place, key_place):
    factor = HEAD_WIDTH ** -0.5
    forward = (((1,), (1,)), ((), ()))
    backward = (((0,), (0,)), ((), ()))
    scores = lax.dot_general(tile_query_rows, block_key_rows, forward, preferred_element_type=jnp.float32) * factor
    scores = jnp.where(key_place[None, :] <= query_place[:, None], scores, -jnp.inf)
    weights = jax.nn.softmax(scores, axis=-1)
    grad_weights = lax.dot_general(gradient_rows, block_value_rows, forward, preferred_element_type=jnp.float32)
    row_delta = jnp.sum(weights * grad_weights, axis=-1, keepdims=True)
    grad_scores = (weights * (grad_weights - row_delta) * factor).astype(jnp.bfloat16)
    query_gradient = jnp.dot(grad_scores, block_key_rows, preferred_element_type=jnp.float32)
    key_gradient = lax.dot_general(grad_scores, tile_query_rows, backward, preferred_element_type=jnp.float32)
    value_gradient = lax.dot_general(weights.astype(jnp.bfloat16), gradient_rows, backward, preferred_element_type=jnp.float32)
    return query_gradient, key_gradient, value_gradient


def reference(queries, keys, values, output_gradient, tile_block_table):
    devices = N_ROW * N_COL
    starting_position = CONTEXT_LENGTH - QROWS
    key_block_grid = keys.reshape(BLOCK_COUNT, BLOCK_KEY_ROWS, KEY_VALUE_HEADS, HEAD_WIDTH)
    value_block_grid = values.reshape(BLOCK_COUNT, BLOCK_KEY_ROWS, KEY_VALUE_HEADS, HEAD_WIDTH)
    row_offsets = jnp.arange(BLOCK_KEY_ROWS, dtype=jnp.int32)
    rows_per_head = jnp.arange(GROUP_WIDTH * TILE_QUERY_ROWS, dtype=jnp.int32) % TILE_QUERY_ROWS

    def tile_step(tile_index):
        block_numbers = tile_block_table[tile_index]
        query_block_tile = lax.dynamic_slice_in_dim(queries, tile_index * TILE_QUERY_ROWS, TILE_QUERY_ROWS, 0)
        tile_gradient = lax.dynamic_slice_in_dim(output_gradient, tile_index * TILE_QUERY_ROWS, TILE_QUERY_ROWS, 0)
        tile_query_rows = query_block_tile.reshape(TILE_QUERY_ROWS, KEY_VALUE_HEADS, GROUP_WIDTH, HEAD_WIDTH).transpose(1, 2, 0, 3).reshape(KEY_VALUE_HEADS, GROUP_WIDTH * TILE_QUERY_ROWS, HEAD_WIDTH)
        gradient_rows = tile_gradient.reshape(TILE_QUERY_ROWS, KEY_VALUE_HEADS, GROUP_WIDTH, HEAD_WIDTH).transpose(1, 2, 0, 3).reshape(KEY_VALUE_HEADS, GROUP_WIDTH * TILE_QUERY_ROWS, HEAD_WIDTH)
        block_key_rows = key_block_grid[block_numbers].transpose(2, 0, 1, 3).reshape(KEY_VALUE_HEADS, PICKED_BLOCKS * BLOCK_KEY_ROWS, HEAD_WIDTH)
        block_value_rows = value_block_grid[block_numbers].transpose(2, 0, 1, 3).reshape(KEY_VALUE_HEADS, PICKED_BLOCKS * BLOCK_KEY_ROWS, HEAD_WIDTH)
        query_place = starting_position + tile_index * TILE_QUERY_ROWS + rows_per_head
        key_place = (block_numbers[:, None] * BLOCK_KEY_ROWS + row_offsets[None, :]).reshape(PICKED_BLOCKS * BLOCK_KEY_ROWS)
        query_gradient, key_gradient, value_gradient = jax.vmap(pair_grads, in_axes=(0, 0, 0, 0, None, None))(
            tile_query_rows, gradient_rows, block_key_rows, block_value_rows, query_place, key_place)
        query_gradient = query_gradient.reshape(KEY_VALUE_HEADS, GROUP_WIDTH, TILE_QUERY_ROWS, HEAD_WIDTH).transpose(2, 0, 1, 3).reshape(TILE_QUERY_ROWS, QUERY_HEADS * HEAD_WIDTH).astype(jnp.bfloat16)
        key_value_terms = jnp.stack((key_gradient, value_gradient), axis=0).reshape(2, KEY_VALUE_HEADS, PICKED_BLOCKS, BLOCK_KEY_ROWS, HEAD_WIDTH)
        key_value_terms = key_value_terms.transpose(2, 3, 0, 1, 4).reshape(PICKED_BLOCKS, BLOCK_KEY_ROWS * 2 * KEY_VALUE_HEADS * HEAD_WIDTH)
        return query_gradient, key_value_terms

    def per_device_body(running_totals, device):
        tile_range = device * DEVICE_TILES + jnp.arange(DEVICE_TILES, dtype=jnp.int32)
        query_gradient, key_value_terms = lax.map(tile_step, tile_range)
        block_numbers = lax.dynamic_slice_in_dim(tile_block_table, device * DEVICE_TILES, DEVICE_TILES, 0).reshape(DEVICE_TILES * PICKED_BLOCKS)
        paired_terms = key_value_terms.reshape(DEVICE_TILES * PICKED_BLOCKS, BLOCK_KEY_ROWS * 2 * KEY_VALUE_HEADS * HEAD_WIDTH)
        same_block = (block_numbers[:, None] == block_numbers[None, :]).astype(jnp.float32)
        first_seen = (jnp.sum(jnp.tril(same_block, -1), axis=1) == 0).astype(jnp.float32)
        merged = jnp.dot(same_block, paired_terms, precision=lax.Precision.HIGHEST, preferred_element_type=jnp.float32)
        rounded = lax.optimization_barrier(merged.astype(jnp.bfloat16)).astype(jnp.float32) * first_seen[:, None]
        running_totals = running_totals.at[block_numbers].add(rounded)
        return running_totals, query_gradient

    running_totals, query_gradients = lax.scan(per_device_body, jnp.zeros((BLOCK_COUNT, BLOCK_KEY_ROWS * 2 * KEY_VALUE_HEADS * HEAD_WIDTH), jnp.float32),
                                    jnp.arange(devices, dtype=jnp.int32))
    dqueries = query_gradients.reshape(QROWS, QUERY_HEADS * HEAD_WIDTH)
    overall_row_count = running_totals.reshape(CONTEXT_LENGTH, 2 * KEY_VALUE_HEADS * HEAD_WIDTH)
    return dqueries, overall_row_count[:, :KEY_VALUE_HEADS * HEAD_WIDTH].astype(jnp.bfloat16), overall_row_count[:, KEY_VALUE_HEADS * HEAD_WIDTH:].astype(jnp.bfloat16)
```

```python
import math

import jax
import jax.numpy as jnp
from jax import lax
from jax.experimental import pallas as pl
from jax.experimental.pallas import tpu as pltpu
from jax.sharding import PartitionSpec as P

HEAD_WIDTH = 128
GROUP_WIDTH = 16
TILE_QUERY_ROWS = 128
BLOCK_KEY_ROWS = 512
PICKED_BLOCKS = 3
HEADS_STEP = 8
SCALE = HEAD_WIDTH**-0.5
SCALE_LOG2 = SCALE * math.log2(math.e)
ROWS_ROWS = (((1,), (1,)), ((), ()))
AXES = ("row", "col")

F32 = jnp.float32
BF16 = jnp.bfloat16


class Layout:
    def __init__(self, mesh):
        self.n_row = mesh.shape["row"]
        self.n_col = mesh.shape["col"]
        self.ny = 1
        while self.n_row % (2 * self.ny) == 0 and 4 * self.ny * self.ny <= self.n_row:
            self.ny *= 2
        self.nz = self.n_row // self.ny
        self.plane = self.ny * self.n_col

    def device(self, z, y, c):
        return (z * self.ny + y) * self.n_col + c

    def everyone(self):
        return [
            (z, y, c) for z in range(self.nz) for y in range(self.ny) for c in range(self.n_col)
        ]

    def along_z(self, k):
        return [
            (self.device(z, y, c), self.device((z + k) % self.nz, y, c))
            for z, y, c in self.everyone()
        ]

    def in_plane(self, j):
        jy, jc = divmod(j, self.n_col)
        return [
            (self.device(z, y, c), self.device(z, (y + jy) % self.ny, (c + jc) % self.n_col))
            for z, y, c in self.everyone()
        ]


def wrap(value, size):
    return lax.rem(value + size, size)


def wanted_row(tables, plane_index, column, n_col):
    row = jnp.int32(-1)
    for entry in range(tables.shape[1]):
        block = tables[plane_index, entry]
        row = jnp.where(lax.rem(block, n_col) == column, block // n_col, row)
    return row


def select_kernel(lay, place, tables, *refs):
    gathered, outs = refs[: lay.nz], refs[lay.nz :]
    z, y, c = place[0], place[1], place[2]
    for j in range(lay.plane):
        jy, jc = divmod(j, lay.n_col)
        other = wrap(y + jy, lay.ny) * lay.n_col + wrap(c + jc, lay.n_col)
        row = wanted_row(tables, other, c, lay.n_col)
        hops = wrap(z - jnp.maximum(row, 0) // lay.ny, lay.nz)
        for k in range(lay.nz):

            @pl.when(hops == k)
            def _(k=k):
                outs[j][...] = gathered[k][...]


def select_units(lay, place, tables, gathered):
    unit = gathered[0]
    return pl.pallas_call(
        lambda *refs: select_kernel(lay, *refs),
        out_shape=[jax.ShapeDtypeStruct(unit.shape, unit.dtype)] * lay.plane,
        in_specs=[pl.BlockSpec(memory_space=pltpu.SMEM)] * 2
        + [pl.BlockSpec(memory_space=pltpu.VMEM)] * lay.nz,
        out_specs=[pl.BlockSpec(memory_space=pltpu.VMEM)] * lay.plane,
        name="select_units",
    )(place, tables, *gathered)


def combine_kernel(lay, place, tables, *refs):
    parts, outs, acc = refs[: lay.plane], refs[lay.plane : lay.plane + lay.nz], refs[-1]
    z, y, c = place[0], place[1], place[2]
    acc[...] = jnp.zeros_like(acc)
    for j in range(lay.plane):
        jy, jc = divmod(j, lay.n_col)
        other = wrap(y - jy, lay.ny) * lay.n_col + wrap(c - jc, lay.n_col)
        row = wanted_row(tables, other, c, lay.n_col)
        ahead = wrap(jnp.maximum(row, 0) // lay.ny - z, lay.nz)

        @pl.when((row >= 0) & (lax.rem(jnp.maximum(row, 0), lay.ny) == y))
        def _(j=j, ahead=ahead):
            acc[ahead] += parts[j][...].astype(F32)

    for k in range(lay.nz):
        outs[k][...] = acc[k].astype(BF16)


def combine_parts(lay, place, tables, parts):
    unit = parts[0]
    return pl.pallas_call(
        lambda *refs: combine_kernel(lay, *refs),
        out_shape=[jax.ShapeDtypeStruct(unit.shape, unit.dtype)] * lay.nz,
        in_specs=[pl.BlockSpec(memory_space=pltpu.SMEM)] * 2
        + [pl.BlockSpec(memory_space=pltpu.VMEM)] * lay.plane,
        out_specs=[pl.BlockSpec(memory_space=pltpu.VMEM)] * lay.nz,
        scratch_shapes=[pltpu.VMEM((lay.nz,) + unit.shape, F32)],
        name="combine_parts",
    )(place, tables, *parts)


def grads_kernel(lay, n_in, place, lists, q, do, *refs):
    units = refs[: lay.plane]
    outs = refs[n_in:]
    dq, part_refs = outs[0], outs[1 : 1 + lay.n_col]
    kv, kt, acc, sems = outs[1 + lay.n_col :]
    y, c, tile0, start = place[1], place[2], place[3], place[4]
    t = pl.program_id(0)
    n_tiles = lists.shape[0]
    head = HEAD_WIDTH
    rows = HEADS_STEP * TILE_QUERY_ROWS

    def slot_of(block):
        return wrap(lax.rem(block, lay.n_col) - c, lay.n_col)

    @pl.when(t == 0)
    def _():
        acc[...] = jnp.zeros_like(acc)
        kv[...] = jnp.zeros_like(kv)
        for j in range(lay.plane):
            jy, jc = divmod(j, lay.n_col)
            from_y, from_c = wrap(y - jy, lay.ny), wrap(c - jc, lay.n_col)
            needed = jnp.bool_(False)
            for tile in range(n_tiles):
                for pick in range(PICKED_BLOCKS):
                    block = lists[tile, pick]
                    needed |= (lax.rem(block, lay.n_col) == from_c) & (
                        lax.rem(block // lay.n_col, lay.ny) == from_y
                    )

            @pl.when(needed)
            def _(j=j, from_c=from_c):
                copy = pltpu.make_async_copy(units[j], kv.at[slot_of(from_c)], sems)
                copy.start()
                copy.wait()

        for s in range(lay.n_col):
            kt[s] = kv[s, :, :head].T

    slots = [slot_of(lists[t, pick]) for pick in range(PICKED_BLOCKS)]
    offset = start + (tile0 + t) * TILE_QUERY_ROWS - lists[t, 0] * BLOCK_KEY_ROWS

    def step(i, carry):
        base = pl.multiple_of(i * rows, rows)
        q_rows = jnp.concatenate([q[:, pl.ds(base + h * head, head)] for h in range(HEADS_STEP)], 0)
        do_rows = jnp.concatenate(
            [do[:, pl.ds(base + h * head, head)] for h in range(HEADS_STEP)], 0
        )
        scores = [
            lax.dot_general(kv[s, :, :head], q_rows, ROWS_ROWS, preferred_element_type=F32)
            for s in slots
        ]
        key_at = lax.broadcasted_iota(jnp.int32, (BLOCK_KEY_ROWS, rows), 0)
        query_at = (
            lax.rem(
                lax.broadcasted_iota(jnp.int32, (BLOCK_KEY_ROWS, rows), 1),
                jnp.int32(TILE_QUERY_ROWS),
            )
            + offset
        )
        scores[0] = jnp.where(key_at <= query_at, scores[0], -jnp.inf)
        top = jnp.max(scores[0], axis=0, keepdims=True)
        for s in scores[1:]:
            top = jnp.maximum(top, jnp.max(s, axis=0, keepdims=True))
        top = top * SCALE_LOG2
        exps = [jnp.exp2(s * SCALE_LOG2 - top) for s in scores]
        gw = [
            lax.dot_general(kv[s, :, head:], do_rows, ROWS_ROWS, preferred_element_type=F32)
            for s in slots
        ]
        inverse = 1.0 / sum(jnp.sum(e, axis=0, keepdims=True) for e in exps)
        delta = inverse * sum(jnp.sum(e * g, axis=0, keepdims=True) for e, g in zip(exps, gw))
        dq_t = jnp.zeros((head, rows), F32)
        for s, e, g in zip(slots, exps, gw):
            weights = e * inverse
            gs = (weights * ((g - delta) * SCALE)).astype(BF16)
            acc[s, :, :head] += jnp.dot(gs, q_rows, preferred_element_type=F32)
            acc[s, :, head:] += jnp.dot(
                weights.astype(BF16), do_rows, preferred_element_type=F32
            )
            dq_t += jnp.dot(kt[s], gs, preferred_element_type=F32)
        for h in range(HEADS_STEP):
            dq[:, pl.ds(base + h * head, head)] = (
                dq_t[:, h * TILE_QUERY_ROWS : (h + 1) * TILE_QUERY_ROWS].T.astype(BF16)
            )
        return carry

    lax.fori_loop(0, GROUP_WIDTH // HEADS_STEP, step, 0)

    @pl.when(t == n_tiles - 1)
    def _():
        for s in range(lay.n_col):
            part_refs[s][...] = acc[s].astype(BF16)


def group_grads(lay, g, place, lists, queries, output_gradient, units, dq_in):
    width = GROUP_WIDTH * HEAD_WIDTH
    wide = pl.BlockSpec((TILE_QUERY_ROWS, width), lambda t, *_: (t, g))
    unit = units[0].shape
    aliased = [] if dq_in is None else [dq_in]
    n_in = lay.plane + len(aliased)
    flops = 10 * queries.shape[0] * width * PICKED_BLOCKS * BLOCK_KEY_ROWS
    return pl.pallas_call(
        lambda *refs: grads_kernel(lay, n_in, *refs),
        out_shape=[jax.ShapeDtypeStruct(queries.shape, BF16)]
        + [jax.ShapeDtypeStruct(unit, BF16)] * lay.n_col,
        grid_spec=pltpu.PrefetchScalarGridSpec(
            num_scalar_prefetch=2,
            grid=(lists.shape[0],),
            in_specs=[wide, wide] + [pl.BlockSpec(memory_space=pl.ANY)] * n_in,
            out_specs=[wide] + [pl.BlockSpec(unit, lambda t, *_: (0, 0))] * lay.n_col,
            scratch_shapes=[
                pltpu.VMEM((lay.n_col,) + unit, BF16),
                pltpu.VMEM((lay.n_col, HEAD_WIDTH, BLOCK_KEY_ROWS), BF16),
                pltpu.VMEM((lay.n_col,) + unit, F32),
                pltpu.SemaphoreType.DMA,
            ],
        ),
        input_output_aliases={} if dq_in is None else {4 + lay.plane: 0},
        compiler_params=pltpu.CompilerParams(
            dimension_semantics=("arbitrary",), vmem_limit_bytes=60 << 20
        ),
        cost_estimate=pl.CostEstimate(
            flops=flops, bytes_accessed=6 * queries.shape[0] * width, transcendentals=0
        ),
        name=f"group_grads_{g}",
    )(place, lists, queries, output_gradient, *units, *aliased)


def local(lay, queries, keys, values, output_gradient, tile_block_table):
    n_tiles = tile_block_table.shape[0]
    groups = keys.shape[1] // HEAD_WIDTH
    row, col = lax.axis_index("row"), lax.axis_index("col")
    me = row * lay.n_col + col
    devices = lay.n_row * lay.n_col
    start = devices * (keys.shape[0] - n_tiles * TILE_QUERY_ROWS)
    place = jnp.stack(
        [row // lay.ny, lax.rem(row, lay.ny), col, me * n_tiles, jnp.int32(start)]
    ).astype(jnp.int32)

    def cut(array, g):
        return array[:, g * HEAD_WIDTH : (g + 1) * HEAD_WIDTH]

    gathered = []
    for g in range(groups):
        unit = jnp.concatenate((cut(keys, g), cut(values, g)), axis=1)
        gathered.append(
            [unit] + [lax.ppermute(unit, AXES, lay.along_z(k)) for k in range(1, lay.nz)]
        )
    flat = tile_block_table.reshape(1, n_tiles * PICKED_BLOCKS)
    tables = lax.all_gather(flat, "col", axis=0, tiled=True)
    tables = jnp.stack(
        [tables]
        + [
            lax.ppermute(tables, AXES, lay.in_plane(jy * lay.n_col)) for jy in range(1, lay.ny)
        ]
    )
    order = wrap(place[1] - jnp.arange(lay.ny, dtype=jnp.int32), lay.ny)
    tables = jnp.take(tables, order, axis=0).reshape(lay.plane, n_tiles * PICKED_BLOCKS)

    landed = []
    for g in range(groups):
        units = select_units(lay, place, tables, gathered[g])
        landed.append(
            [units[0]]
            + [lax.ppermute(units[j], AXES, lay.in_plane(j)) for j in range(1, lay.plane)]
        )
    dq = None
    sums = []
    for g in range(groups):
        dq, *parts = group_grads(
            lay, g, place, tile_block_table, queries, output_gradient, landed[g], dq
        )
        arrived = [parts[0]] + [
            lax.ppermute(parts[j % lay.n_col], AXES, lay.in_plane(j)) for j in range(1, lay.plane)
        ]
        mine = combine_parts(lay, place, tables, arrived)
        total = mine[0].astype(F32)
        for k in range(1, lay.nz):
            total += lax.ppermute(mine[k], AXES, lay.along_z(k)).astype(F32)
        sums.append(total.astype(BF16))
    dkeys = jnp.concatenate([s[:, :HEAD_WIDTH] for s in sums], axis=1)
    dvalues = jnp.concatenate([s[:, HEAD_WIDTH:] for s in sums], axis=1)
    return dq, dkeys, dvalues


def solution(mesh):
    lay = Layout(mesh)
    spec = P(AXES, None)
    return jax.shard_map(
        lambda *args: local(lay, *args),
        mesh=mesh,
        in_specs=(spec,) * 5,
        out_specs=(spec,) * 3,
        check_vma=False,
    )
```

```python
import functools
import math

import jax
import jax.numpy as jnp
from jax import lax
from jax.experimental import pallas as pl
from jax.experimental.pallas import tpu as pltpu
from jax.sharding import PartitionSpec as P

HEAD_WIDTH = 128
GROUP_WIDTH = 16
TILE_QUERY_ROWS = 128
BLOCK_KEY_ROWS = 512
PICKED_BLOCKS = 3
HEADS_STEP = 8
SCALE = HEAD_WIDTH**-0.5
SCALE_LOG2 = SCALE * math.log2(math.e)
ROWS_ROWS = (((1,), (1,)), ((), ()))
VMEM_GRANT = 67043328
AXES = ("row", "col")

F32 = jnp.float32
BF16 = jnp.bfloat16


class Layout:
    def __init__(self, mesh):
        self.n_row = mesh.shape["row"]
        self.n_col = mesh.shape["col"]
        self.ny = 1
        while self.n_row % (2 * self.ny) == 0 and 4 * self.ny * self.ny <= self.n_row:
            self.ny *= 2
        self.nz = self.n_row // self.ny
        self.plane = self.ny * self.n_col
        self.col_bits = self.n_col.bit_length() - 1
        self.y_bits = self.ny.bit_length() - 1
        assert self.n_col == 1 << self.col_bits and self.n_row == self.nz << self.y_bits

    def col_of(self, block):
        return block & (self.n_col - 1)

    def y_of(self, block):
        return (block >> self.col_bits) & (self.ny - 1)

    def ahead(self, y, c, j):
        jy, jc = divmod(j, self.n_col)
        return wrap(y + jy, self.ny) * self.n_col + wrap(c + jc, self.n_col)

    def behind(self, y, c, j):
        jy, jc = divmod(j, self.n_col)
        return wrap(y - jy, self.ny) * self.n_col + wrap(c - jc, self.n_col)

    def plane_groups(self):
        return [
            [self.device(z, y, c) for y in range(self.ny) for c in range(self.n_col)]
            for z in range(self.nz)
        ]

    def z_of(self, block):
        return block >> (self.col_bits + self.y_bits)

    def device(self, z, y, c):
        return (z * self.ny + y) * self.n_col + c

    def everyone(self):
        return [
            (z, y, c) for z in range(self.nz) for y in range(self.ny) for c in range(self.n_col)
        ]

    def along_z(self, k):
        return [
            (self.device(z, y, c), self.device((z + k) % self.nz, y, c))
            for z, y, c in self.everyone()
        ]

    def in_plane(self, j):
        jy, jc = divmod(j, self.n_col)
        return [
            (self.device(z, y, c), self.device(z, (y + jy) % self.ny, (c + jc) % self.n_col))
            for z, y, c in self.everyone()
        ]


def wrap(value, size):
    return jnp.where(value >= size, value - size, jnp.where(value < 0, value + size, value))


def hbm(count):
    return [pl.BlockSpec(memory_space=pltpu.HBM)] * count


def smem(count):
    return [pl.BlockSpec(memory_space=pltpu.SMEM)] * count


def plan_kernel(lay, place, *refs):
    tables, (send, keep) = refs[: lay.ny], refs[lay.ny :]
    z, y, c = place[0], place[1], place[2]

    def wanted(table, device_col):
        block = jnp.int32(-1)
        for entry in range(table.shape[1]):
            named = table[device_col, entry]
            block = jnp.where((lay.col_of(named) == c) & (lay.y_of(named) == y), named, block)
        return block

    for j in range(lay.plane):
        jy, jc = divmod(j, lay.n_col)
        block = wanted(tables[(lay.ny - jy) % lay.ny], wrap(c + jc, lay.n_col))
        send[j] = jnp.where(block >= 0, wrap(z - lay.z_of(block), lay.nz), 0)
        block = wanted(tables[jy], wrap(c - jc, lay.n_col))
        keep[j] = jnp.where(block >= 0, wrap(lay.z_of(block) - z, lay.nz), -1)


def make_plan(lay, place, tables):
    count = jax.ShapeDtypeStruct((lay.plane,), jnp.int32)
    return pl.pallas_call(
        lambda *refs: plan_kernel(lay, *refs),
        out_shape=[count] * 2,
        in_specs=smem(1 + lay.ny),
        out_specs=smem(2),
        compiler_params=pltpu.CompilerParams(vmem_limit_bytes=VMEM_GRANT),
        name="make_plan",
    )(place, *tables)


def select_kernel(lay, joined, place, send, *refs):
    sources = refs[-3].shape[0]
    gathered, outs = refs[:sources], refs[sources:-3]
    held, in_sems, out_sems = refs[-3:]
    y, c = place[1], place[2]
    loads = [
        pltpu.make_async_copy(gathered[k], held.at[k], in_sems.at[k]) for k in range(sources)
    ]
    for load in loads:
        load.start()
    for load in loads:
        load.wait()
    stores = []
    for j in range(lay.plane):
        target = outs[0].at[lay.ahead(y, c, j)] if joined else outs[j]
        stores.append(pltpu.make_async_copy(held.at[send[j]], target, out_sems.at[j]))
    for store in stores:
        store.start()
    for store in stores:
        store.wait()


def select_units(lay, place, send, gathered, joined):
    unit = gathered[0]
    out = jax.ShapeDtypeStruct(((lay.plane,) if joined else ()) + unit.shape, unit.dtype)
    count = 1 if joined else lay.plane
    return pl.pallas_call(
        lambda *refs: select_kernel(lay, joined, *refs),
        out_shape=[out] * count,
        in_specs=smem(2) + hbm(len(gathered)),
        out_specs=hbm(count),
        scratch_shapes=[
            pltpu.VMEM((len(gathered),) + unit.shape, unit.dtype),
            pltpu.SemaphoreType.DMA((len(gathered),)),
            pltpu.SemaphoreType.DMA((lay.plane,)),
        ],
        compiler_params=pltpu.CompilerParams(vmem_limit_bytes=VMEM_GRANT),
        name="select_units",
    )(place, send, *gathered)


def combine_kernel(lay, n_parts, place, keep, *refs):
    parts, outs = refs[:n_parts], refs[n_parts : n_parts + lay.nz]
    held, acc, sems = refs[n_parts + lay.nz :]
    y, c = place[1], place[2]
    loads = []
    for j in range(lay.plane):
        source = parts[0].at[lay.behind(y, c, j)] if n_parts == 1 else parts[j]
        loads.append(pltpu.make_async_copy(source, held.at[j], sems.at[j]))
    for j in range(lay.plane):

        @pl.when(keep[j] >= 0)
        def _(j=j):
            loads[j].start()

    acc[...] = jnp.zeros_like(acc)
    for j in range(lay.plane):

        @pl.when(keep[j] >= 0)
        def _(j=j):
            loads[j].wait()
            acc[keep[j]] += held[j].astype(F32)

    for k in range(lay.nz):
        outs[k][...] = acc[k].astype(BF16)


def combine_parts(lay, place, keep, parts):
    joined = not isinstance(parts, list)
    parts = [parts] if joined else parts
    unit = jax.ShapeDtypeStruct(parts[0].shape[-2:], parts[0].dtype)
    return pl.pallas_call(
        lambda *refs: combine_kernel(lay, len(parts), *refs),
        out_shape=[jax.ShapeDtypeStruct(unit.shape, unit.dtype)] * lay.nz,
        in_specs=smem(2) + hbm(len(parts)),
        out_specs=[pl.BlockSpec(memory_space=pltpu.VMEM)] * lay.nz,
        scratch_shapes=[
            pltpu.VMEM((lay.plane,) + unit.shape, unit.dtype),
            pltpu.VMEM((lay.nz,) + unit.shape, F32),
            pltpu.SemaphoreType.DMA((lay.plane,)),
        ],
        compiler_params=pltpu.CompilerParams(vmem_limit_bytes=VMEM_GRANT),
        name="combine_parts",
    )(place, keep, *parts)


def total_kernel(lay, widths, *refs):
    terms, (dkeys, dvalues) = refs[:-2], refs[-2:]
    for n, pieces in enumerate(widths):
        total = terms[n * lay.nz][...].astype(F32)
        for k in range(1, lay.nz):
            total += terms[n * lay.nz + k][...].astype(F32)
        total = total.astype(BF16)
        for piece, (which, g) in enumerate(pieces):
            out = (dkeys, dvalues)[which]
            out[:, g * HEAD_WIDTH : (g + 1) * HEAD_WIDTH] = total[
                :, piece * HEAD_WIDTH : (piece + 1) * HEAD_WIDTH
            ]


def total_up(lay, sums, shape):
    terms = [term for _, received in sums for term in received]
    return pl.pallas_call(
        lambda *refs: total_kernel(lay, [pieces for pieces, _ in sums], *refs),
        out_shape=[jax.ShapeDtypeStruct(shape, BF16)] * 2,
        in_specs=[pl.BlockSpec(memory_space=pltpu.VMEM)] * len(terms),
        out_specs=[pl.BlockSpec(memory_space=pltpu.VMEM)] * 2,
        compiler_params=pltpu.CompilerParams(vmem_limit_bytes=VMEM_GRANT),
        name="total_up",
    )(*terms)


def grads_kernel(lay, spec, place, lists, q, do, *refs):
    first, last, n_units, has_dq, has_carry, emit = spec
    units, refs = refs[:n_units], refs[n_units + has_dq :]
    carry, refs = (refs[0], refs[1:]) if has_carry else (None, refs)
    n_out = {"carry": 1, "joined": 1, "split": 2 * lay.n_col}[emit]
    dq, outs, refs = refs[0], refs[1 : 1 + n_out], refs[1 + n_out :]
    k_rows, v_rows, kt, acc, parts, sems, carry_sem, part_sems = refs
    y, c, tile0, start = place[1], place[2], place[3], place[4]
    t = pl.program_id(0) + first
    head = HEAD_WIDTH
    rows = HEADS_STEP * TILE_QUERY_ROWS

    @pl.when(t == first)
    def _():
        if has_carry:
            carried = pltpu.make_async_copy(carry, acc, carry_sem)
            carried.start()
        copies = []
        for column in range(lay.n_col):
            block = jnp.int32(-1)
            for tile in range(first, last):
                for pick in range(PICKED_BLOCKS):
                    named = lists[tile, pick]
                    block = jnp.where(lay.col_of(named) == column, named, block)
            from_y = lay.y_of(block)
            if n_units == 1:
                here = units[0].at[from_y * lay.n_col + column]
                pairs = [(block >= 0, [here.at[:, :head], here.at[:, head:]])]
            else:
                hops = wrap(y - from_y, lay.ny) * lay.n_col + wrap(c - column, lay.n_col)
                pairs = [
                    ((block >= 0) & (hops == j), [units[j].at[:, :head], units[j].at[:, head:]])
                    for j in range(lay.plane)
                ]
            for needed, sources in pairs:
                for n, (source, target) in enumerate(zip(sources, (k_rows, v_rows))):
                    copy = pltpu.make_async_copy(source, target.at[column], sems.at[n, column])
                    copies.append((needed, copy))
        for needed, copy in copies:
            pl.when(needed)(copy.start)
        if not has_carry:
            acc[...] = jnp.zeros_like(acc)
        for needed, copy in copies:
            pl.when(needed)(copy.wait)
        for column in range(lay.n_col):
            kt[column] = k_rows[column].T
        if has_carry:
            carried.wait()

    slots = [lay.col_of(lists[t, pick]) for pick in range(PICKED_BLOCKS)]
    offset = start + (tile0 + t) * TILE_QUERY_ROWS - lists[t, 0] * BLOCK_KEY_ROWS

    def step(own_rows, i, carry_value):
        base = pl.multiple_of(i * rows, rows)
        q_rows = jnp.concatenate([q[:, pl.ds(base + h * head, head)] for h in range(HEADS_STEP)], 0)
        do_rows = jnp.concatenate(
            [do[:, pl.ds(base + h * head, head)] for h in range(HEADS_STEP)], 0
        )
        seen = [own_rows] + [BLOCK_KEY_ROWS] * (PICKED_BLOCKS - 1)
        scores = [
            lax.dot_general(k_rows[s, :n], q_rows, ROWS_ROWS, preferred_element_type=F32)
            for s, n in zip(slots, seen)
        ]
        key_at = lax.broadcasted_iota(jnp.int32, (own_rows, rows), 0)
        query_at = lax.broadcasted_iota(jnp.int32, (own_rows, rows), 1)
        query_at = (query_at & (TILE_QUERY_ROWS - 1)) + offset
        scores[0] = jnp.where(key_at <= query_at, scores[0], -jnp.inf)
        top = jnp.max(scores[0], axis=0, keepdims=True)
        for s in scores[1:]:
            top = jnp.maximum(top, jnp.max(s, axis=0, keepdims=True))
        top = top * SCALE_LOG2
        exps = [jnp.exp2(s * SCALE_LOG2 - top) for s in scores]
        gw = [
            lax.dot_general(v_rows[s, :n], do_rows, ROWS_ROWS, preferred_element_type=F32)
            for s, n in zip(slots, seen)
        ]
        inverse = 1.0 / sum(jnp.sum(e, axis=0, keepdims=True) for e in exps)
        delta = inverse * sum(jnp.sum(e * g, axis=0, keepdims=True) for e, g in zip(exps, gw))
        dq_t = jnp.zeros((head, rows), F32)
        for s, n, e, g in zip(slots, seen, exps, gw):
            weights = e * inverse
            gs = (weights * ((g - delta) * SCALE)).astype(BF16)
            acc[s, :n, :head] += jnp.dot(gs, q_rows, preferred_element_type=F32)
            acc[s, :n, head:] += jnp.dot(
                weights.astype(BF16), do_rows, preferred_element_type=F32
            )
            dq_t += jnp.dot(kt[s, :, :n], gs, preferred_element_type=F32)
        for h in range(HEADS_STEP):
            dq[:, pl.ds(base + h * head, head)] = (
                dq_t[:, h * TILE_QUERY_ROWS : (h + 1) * TILE_QUERY_ROWS].T.astype(BF16)
            )
        return carry_value

    half = BLOCK_KEY_ROWS // 2
    for own_rows, fits in ((half, offset < half), (BLOCK_KEY_ROWS, offset >= half)):

        @pl.when(fits)
        def _(own_rows=own_rows):
            lax.fori_loop(0, GROUP_WIDTH // HEADS_STEP, functools.partial(step, own_rows), 0)

    @pl.when(t == last - 1)
    def _():
        if emit == "carry":
            copy = pltpu.make_async_copy(acc, outs[0], carry_sem)
            copy.start()
            copy.wait()
        elif emit == "joined":
            copies = []
            for column in range(lay.n_col):
                parts[column] = acc[column].astype(BF16)
                for row in range(lay.ny):
                    place_at = row * lay.n_col + column
                    copy = pltpu.make_async_copy(
                        parts.at[column], outs[0].at[place_at], part_sems.at[place_at]
                    )
                    copy.start()
                    copies.append(copy)
            for copy in copies:
                copy.wait()
        else:
            for s in range(lay.n_col):
                column = wrap(c + s, lay.n_col)
                outs[s][...] = acc[column, :, head:].astype(BF16)
                outs[lay.n_col + s][...] = acc[column, :, :head].astype(BF16)


def group_grads(lay, g, tiles, place, lists, queries, output_gradient, units, dq_in, carry, emit):
    first, last = tiles
    width = GROUP_WIDTH * HEAD_WIDTH
    wide = pl.BlockSpec((TILE_QUERY_ROWS, width), lambda t, *_: (t + first, g))
    keys_shape = (BLOCK_KEY_ROWS, HEAD_WIDTH)
    pair_shape = (BLOCK_KEY_ROWS, 2 * HEAD_WIDTH)
    acc_shape = (lay.n_col,) + pair_shape
    flat_units = list(units)
    extra = [x for x in (dq_in, carry) if x is not None]
    spec = (first, last, len(flat_units), int(dq_in is not None), carry is not None, emit)
    shapes = {
        "carry": [(acc_shape, F32)],
        "joined": [((lay.plane,) + pair_shape, BF16)],
        "split": [(keys_shape, BF16)] * (2 * lay.n_col),
    }[emit]
    flops = 10 * TILE_QUERY_ROWS * (last - first) * width * PICKED_BLOCKS * BLOCK_KEY_ROWS
    return pl.pallas_call(
        lambda *refs: grads_kernel(lay, spec, *refs),
        out_shape=[jax.ShapeDtypeStruct(queries.shape, BF16)]
        + [jax.ShapeDtypeStruct(*shape) for shape in shapes],
        grid_spec=pltpu.PrefetchScalarGridSpec(
            num_scalar_prefetch=2,
            grid=(last - first,),
            in_specs=[wide, wide] + hbm(len(flat_units) + len(extra)),
            out_specs=[wide]
            + (
                hbm(1)
                if emit != "split"
                else [pl.BlockSpec(s, lambda t, *_, n=len(s): (0,) * n) for s, _ in shapes]
            ),
            scratch_shapes=[
                pltpu.VMEM((lay.n_col,) + keys_shape, BF16),
                pltpu.VMEM((lay.n_col,) + keys_shape, BF16),
                pltpu.VMEM((lay.n_col, HEAD_WIDTH, BLOCK_KEY_ROWS), BF16),
                pltpu.VMEM(acc_shape, F32),
                pltpu.VMEM(acc_shape, BF16),
                pltpu.SemaphoreType.DMA((2, lay.plane)),
                pltpu.SemaphoreType.DMA,
                pltpu.SemaphoreType.DMA((lay.plane,)),
            ],
        ),
        input_output_aliases={} if dq_in is None else {4 + len(flat_units): 0},
        compiler_params=pltpu.CompilerParams(
            dimension_semantics=("arbitrary",), vmem_limit_bytes=VMEM_GRANT
        ),
        cost_estimate=pl.CostEstimate(
            flops=flops,
            bytes_accessed=6 * TILE_QUERY_ROWS * (last - first) * width,
            transcendentals=0,
        ),
    )(place, lists, queries, output_gradient, *flat_units, *extra)


def local(lay, queries, keys, values, output_gradient, tile_block_table):
    n_tiles = tile_block_table.shape[0]
    groups = keys.shape[1] // HEAD_WIDTH
    row, col = lax.axis_index("row"), lax.axis_index("col")
    me = row * lay.n_col + col
    devices = lay.n_row * lay.n_col
    start = devices * (keys.shape[0] - n_tiles * TILE_QUERY_ROWS)
    place = jnp.stack(
        [row >> lay.y_bits, row & (lay.ny - 1), col, me * n_tiles, jnp.int32(start)]
    ).astype(jnp.int32)

    def cut(array, g):
        return array[:, g * HEAD_WIDTH : (g + 1) * HEAD_WIDTH]

    def gather_z(unit):
        return [unit] + [lax.ppermute(unit, AXES, lay.along_z(k)) for k in range(1, lay.nz)]

    def spread(units):
        return [units[0]] + [
            lax.ppermute(units[j], AXES, lay.in_plane(j)) for j in range(1, lay.plane)
        ]

    def repeat(parts):
        return [parts[j % lay.n_col] for j in range(lay.plane)]

    def exchange(stack):
        return lax.all_to_all(
            stack, AXES, 0, 0, axis_index_groups=lay.plane_groups(), tiled=True
        )

    def finish(mine):
        return [mine[0]] + [lax.ppermute(mine[k], AXES, lay.along_z(k)) for k in range(1, lay.nz)]

    chunks = [[cut(keys, g), cut(values, g)] for g in range(groups)]
    gathered = []
    for chunk in chunks:
        gathered.append(gather_z(jnp.concatenate(chunk, axis=1)))
    flat = tile_block_table.reshape(1, n_tiles * PICKED_BLOCKS)
    table = lax.all_gather(flat, "col", axis=0, tiled=True)
    tables = [table] + [
        lax.ppermute(table, AXES, lay.in_plane(jy * lay.n_col)) for jy in range(1, lay.ny)
    ]
    send, keep = make_plan(lay, place, tables)

    landed = [spread(select_units(lay, place, send, gathered[0], False))]
    landed += [[exchange(select_units(lay, place, send, units, True)[0])] for units in gathered[1:]]
    fixed = (place, tile_block_table, queries, output_gradient)
    sums, waiting, dq = [], [], None
    for g in range(groups):
        emit = "joined" if g < groups - 1 else "split"
        dq, *parts = group_grads(
            lay, g, (0, n_tiles), *fixed, landed[g], dq, None, emit
        )
        if emit == "joined":
            waiting.append((((0, g), (1, g)), exchange(parts[0])))
    arrived, parts = lax.optimization_barrier(([units for _, units in waiting], parts))
    for (pieces, _), units in zip(waiting, arrived):
        sums.append((pieces, finish(combine_parts(lay, place, keep, units))))
    first = spread(repeat(parts[: lay.n_col]))
    second = spread(repeat(parts[lay.n_col :]))
    sums.append((((1, g),), finish(combine_parts(lay, place, keep, first))))
    sums.append((((0, g),), finish(combine_parts(lay, place, keep, second))))
    dkeys, dvalues = total_up(lay, sums, keys.shape)
    return dq, dkeys, dvalues


def solution(mesh):
    lay = Layout(mesh)
    spec = P(AXES, None)


    def body(*args):
        return local(lay, *args)

    return jax.shard_map(
        body, mesh=mesh, in_specs=(spec,) * 5, out_specs=(spec,) * 3, check_vma=False
    )
```

```python
import functools
import math

import jax
import jax.numpy as jnp
from jax import lax
from jax.experimental import pallas as pl
from jax.experimental.pallas import tpu as pltpu
from jax.sharding import PartitionSpec as P

HEAD_WIDTH = 128
GROUP_WIDTH = 16
TILE_QUERY_ROWS = 128
BLOCK_KEY_ROWS = 512
PICKED_BLOCKS = 3
HEADS_STEP = 8
SCALE = HEAD_WIDTH**-0.5
SCALE_LOG2 = SCALE * math.log2(math.e)
ROWS_ROWS = (((1,), (1,)), ((), ()))
VMEM_GRANT = 67043328
AXES = ("row", "col")

F32 = jnp.float32
BF16 = jnp.bfloat16


class Layout:
    def __init__(self, mesh):
        self.n_row = mesh.shape["row"]
        self.n_col = mesh.shape["col"]
        self.ny = 1
        while self.n_row % (2 * self.ny) == 0 and 4 * self.ny * self.ny <= self.n_row:
            self.ny *= 2
        self.nz = self.n_row // self.ny
        self.plane = self.ny * self.n_col
        self.col_bits = self.n_col.bit_length() - 1
        self.y_bits = self.ny.bit_length() - 1
        assert self.n_col == 1 << self.col_bits and self.n_row == self.nz << self.y_bits

    def col_of(self, block):
        return block & (self.n_col - 1)

    def y_of(self, block):
        return (block >> self.col_bits) & (self.ny - 1)

    def ahead(self, y, c, j):
        jy, jc = divmod(j, self.n_col)
        return wrap(y + jy, self.ny) * self.n_col + wrap(c + jc, self.n_col)

    def behind(self, y, c, j):
        jy, jc = divmod(j, self.n_col)
        return wrap(y - jy, self.ny) * self.n_col + wrap(c - jc, self.n_col)

    def plane_groups(self):
        return [
            [self.device(z, y, c) for y in range(self.ny) for c in range(self.n_col)]
            for z in range(self.nz)
        ]

    def z_of(self, block):
        return block >> (self.col_bits + self.y_bits)

    def device(self, z, y, c):
        return (z * self.ny + y) * self.n_col + c

    def everyone(self):
        return [
            (z, y, c) for z in range(self.nz) for y in range(self.ny) for c in range(self.n_col)
        ]

    def along_z(self, k):
        return [
            (self.device(z, y, c), self.device((z + k) % self.nz, y, c))
            for z, y, c in self.everyone()
        ]

    def in_plane(self, j):
        jy, jc = divmod(j, self.n_col)
        return [
            (self.device(z, y, c), self.device(z, (y + jy) % self.ny, (c + jc) % self.n_col))
            for z, y, c in self.everyone()
        ]


def wrap(value, size):
    return jnp.where(value >= size, value - size, jnp.where(value < 0, value + size, value))


def hbm(count):
    return [pl.BlockSpec(memory_space=pltpu.HBM)] * count


def smem(count):
    return [pl.BlockSpec(memory_space=pltpu.SMEM)] * count


def plan_kernel(lay, place, *refs):
    tables, (send, keep) = refs[: lay.ny], refs[lay.ny :]
    z, y, c = place[0], place[1], place[2]

    def wanted(table, device_col):
        block = jnp.int32(-1)
        for entry in range(table.shape[1]):
            named = table[device_col, entry]
            block = jnp.where((lay.col_of(named) == c) & (lay.y_of(named) == y), named, block)
        return block

    for j in range(lay.plane):
        jy, jc = divmod(j, lay.n_col)
        block = wanted(tables[(lay.ny - jy) % lay.ny], wrap(c + jc, lay.n_col))
        send[j] = jnp.where(block >= 0, wrap(z - lay.z_of(block), lay.nz), 0)
        block = wanted(tables[jy], wrap(c - jc, lay.n_col))
        keep[j] = jnp.where(block >= 0, wrap(lay.z_of(block) - z, lay.nz), -1)


def make_plan(lay, place, tables):
    count = jax.ShapeDtypeStruct((lay.plane,), jnp.int32)
    return pl.pallas_call(
        lambda *refs: plan_kernel(lay, *refs),
        out_shape=[count] * 2,
        in_specs=smem(1 + lay.ny),
        out_specs=smem(2),
        compiler_params=pltpu.CompilerParams(vmem_limit_bytes=VMEM_GRANT),
        name="make_plan",
    )(place, *tables)


def select_kernel(lay, joined, place, send, *refs):
    sources = refs[-3].shape[0]
    gathered, outs = refs[:sources], refs[sources:-3]
    held, in_sems, out_sems = refs[-3:]
    y, c = place[1], place[2]
    loads = [
        pltpu.make_async_copy(gathered[k], held.at[k], in_sems.at[k]) for k in range(sources)
    ]
    for load in loads:
        load.start()
    for load in loads:
        load.wait()
    stores = []
    for j in range(lay.plane):
        target = outs[0].at[lay.ahead(y, c, j)] if joined else outs[j]
        stores.append(pltpu.make_async_copy(held.at[send[j]], target, out_sems.at[j]))
    for store in stores:
        store.start()
    for store in stores:
        store.wait()


def select_units(lay, place, send, gathered, joined):
    unit = gathered[0]
    out = jax.ShapeDtypeStruct(((lay.plane,) if joined else ()) + unit.shape, unit.dtype)
    count = 1 if joined else lay.plane
    return pl.pallas_call(
        lambda *refs: select_kernel(lay, joined, *refs),
        out_shape=[out] * count,
        in_specs=smem(2) + hbm(len(gathered)),
        out_specs=hbm(count),
        scratch_shapes=[
            pltpu.VMEM((len(gathered),) + unit.shape, unit.dtype),
            pltpu.SemaphoreType.DMA((len(gathered),)),
            pltpu.SemaphoreType.DMA((lay.plane,)),
        ],
        compiler_params=pltpu.CompilerParams(vmem_limit_bytes=VMEM_GRANT),
        name="select_units",
    )(place, send, *gathered)


def combine_kernel(lay, n_parts, place, keep, *refs):
    parts, outs = refs[:n_parts], refs[n_parts : n_parts + lay.nz]
    held, acc, sems = refs[n_parts + lay.nz :]
    y, c = place[1], place[2]
    loads = []
    for j in range(lay.plane):
        source = parts[0].at[lay.behind(y, c, j)] if n_parts == 1 else parts[j]
        loads.append(pltpu.make_async_copy(source, held.at[j], sems.at[j]))
    for j in range(lay.plane):

        @pl.when(keep[j] >= 0)
        def _(j=j):
            loads[j].start()

    acc[...] = jnp.zeros_like(acc)
    for j in range(lay.plane):

        @pl.when(keep[j] >= 0)
        def _(j=j):
            loads[j].wait()
            acc[keep[j]] += held[j].astype(F32)

    for k in range(lay.nz):
        outs[k][...] = acc[k].astype(BF16)


def combine_parts(lay, place, keep, parts):
    joined = not isinstance(parts, list)
    parts = [parts] if joined else parts
    unit = jax.ShapeDtypeStruct(parts[0].shape[-2:], parts[0].dtype)
    return pl.pallas_call(
        lambda *refs: combine_kernel(lay, len(parts), *refs),
        out_shape=[jax.ShapeDtypeStruct(unit.shape, unit.dtype)] * lay.nz,
        in_specs=smem(2) + hbm(len(parts)),
        out_specs=[pl.BlockSpec(memory_space=pltpu.VMEM)] * lay.nz,
        scratch_shapes=[
            pltpu.VMEM((lay.plane,) + unit.shape, unit.dtype),
            pltpu.VMEM((lay.nz,) + unit.shape, F32),
            pltpu.SemaphoreType.DMA((lay.plane,)),
        ],
        compiler_params=pltpu.CompilerParams(vmem_limit_bytes=VMEM_GRANT),
        name="combine_parts",
    )(place, keep, *parts)


def total_kernel(lay, widths, *refs):
    terms, (dkeys, dvalues) = refs[:-2], refs[-2:]
    for n, pieces in enumerate(widths):
        total = terms[n * lay.nz][...].astype(F32)
        for k in range(1, lay.nz):
            total += terms[n * lay.nz + k][...].astype(F32)
        total = total.astype(BF16)
        for piece, (which, g) in enumerate(pieces):
            out = (dkeys, dvalues)[which]
            out[:, g * HEAD_WIDTH : (g + 1) * HEAD_WIDTH] = total[
                :, piece * HEAD_WIDTH : (piece + 1) * HEAD_WIDTH
            ]


def total_up(lay, sums, shape):
    terms = [term for _, received in sums for term in received]
    return pl.pallas_call(
        lambda *refs: total_kernel(lay, [pieces for pieces, _ in sums], *refs),
        out_shape=[jax.ShapeDtypeStruct(shape, BF16)] * 2,
        in_specs=[pl.BlockSpec(memory_space=pltpu.VMEM)] * len(terms),
        out_specs=[pl.BlockSpec(memory_space=pltpu.VMEM)] * 2,
        compiler_params=pltpu.CompilerParams(vmem_limit_bytes=VMEM_GRANT),
        name="total_up",
    )(*terms)


def grads_kernel(lay, spec, place, lists, q, do, *refs):
    first, last, n_units, has_dq, has_carry, emit = spec
    units, refs = refs[:n_units], refs[n_units + has_dq :]
    carry, refs = (refs[0], refs[1:]) if has_carry else (None, refs)
    n_out = {"carry": 1, "joined": 1, "split": 2 * lay.n_col}[emit]
    dq, outs, refs = refs[0], refs[1 : 1 + n_out], refs[1 + n_out :]
    k_rows, v_rows, kt, acc, parts, sems, carry_sem, part_sems = refs
    y, c, tile0, start = place[1], place[2], place[3], place[4]
    t = pl.program_id(0) + first
    head = HEAD_WIDTH
    rows = HEADS_STEP * TILE_QUERY_ROWS

    @pl.when(t == first)
    def _():
        if has_carry:
            carried = pltpu.make_async_copy(carry, acc, carry_sem)
            carried.start()
        copies = []
        for column in range(lay.n_col):
            block = jnp.int32(-1)
            for tile in range(first, last):
                for pick in range(PICKED_BLOCKS):
                    named = lists[tile, pick]
                    block = jnp.where(lay.col_of(named) == column, named, block)
            from_y = lay.y_of(block)
            hops = wrap(y - from_y, lay.ny) * lay.n_col + wrap(c - column, lay.n_col)
            pairs = []
            for j in range(lay.plane):
                needed = (block >= 0) & (hops == j)
                if n_units == lay.plane:
                    pairs.append((needed, 0, units[j].at[:, :head], k_rows))
                    pairs.append((needed, 1, units[j].at[:, head:], v_rows))
                else:
                    pairs.append((needed, 0, units[j], k_rows))
            if n_units > lay.plane:
                here = units[lay.plane].at[from_y * lay.n_col + column]
                pairs.append((block >= 0, 1, here, v_rows))
            for needed, n, source, target in pairs:
                copy = pltpu.make_async_copy(source, target.at[column], sems.at[n, column])
                copies.append((needed, copy))
        for needed, copy in copies:
            pl.when(needed)(copy.start)
        if not has_carry:
            acc[...] = jnp.zeros_like(acc)
        for needed, copy in copies:
            pl.when(needed)(copy.wait)
        for column in range(lay.n_col):
            kt[column] = k_rows[column].T
        if has_carry:
            carried.wait()

    slots = [lay.col_of(lists[t, pick]) for pick in range(PICKED_BLOCKS)]
    offset = start + (tile0 + t) * TILE_QUERY_ROWS - lists[t, 0] * BLOCK_KEY_ROWS

    def step(own_rows, i, carry_value):
        base = pl.multiple_of(i * rows, rows)
        q_rows = jnp.concatenate([q[:, pl.ds(base + h * head, head)] for h in range(HEADS_STEP)], 0)
        do_rows = jnp.concatenate(
            [do[:, pl.ds(base + h * head, head)] for h in range(HEADS_STEP)], 0
        )
        seen = [own_rows] + [BLOCK_KEY_ROWS] * (PICKED_BLOCKS - 1)
        scores = [
            lax.dot_general(k_rows[s, :n], q_rows, ROWS_ROWS, preferred_element_type=F32)
            for s, n in zip(slots, seen)
        ]
        key_at = lax.broadcasted_iota(jnp.int32, (own_rows, rows), 0)
        query_at = lax.broadcasted_iota(jnp.int32, (own_rows, rows), 1)
        query_at = (query_at & (TILE_QUERY_ROWS - 1)) + offset
        scores[0] = jnp.where(key_at <= query_at, scores[0], -jnp.inf)
        top = jnp.max(scores[0], axis=0, keepdims=True)
        for s in scores[1:]:
            top = jnp.maximum(top, jnp.max(s, axis=0, keepdims=True))
        top = top * SCALE_LOG2
        exps = [jnp.exp2(s * SCALE_LOG2 - top) for s in scores]
        gw = [
            lax.dot_general(v_rows[s, :n], do_rows, ROWS_ROWS, preferred_element_type=F32)
            for s, n in zip(slots, seen)
        ]
        inverse = 1.0 / sum(jnp.sum(e, axis=0, keepdims=True) for e in exps)
        delta = inverse * sum(jnp.sum(e * g, axis=0, keepdims=True) for e, g in zip(exps, gw))
        dq_t = jnp.zeros((head, rows), F32)
        for s, n, e, g in zip(slots, seen, exps, gw):
            weights = e * inverse
            gs = (weights * ((g - delta) * SCALE)).astype(BF16)
            acc[s, :n, :head] += jnp.dot(gs, q_rows, preferred_element_type=F32)
            acc[s, :n, head:] += jnp.dot(
                weights.astype(BF16), do_rows, preferred_element_type=F32
            )
            dq_t += jnp.dot(kt[s, :, :n], gs, preferred_element_type=F32)
        for h in range(HEADS_STEP):
            dq[:, pl.ds(base + h * head, head)] = (
                dq_t[:, h * TILE_QUERY_ROWS : (h + 1) * TILE_QUERY_ROWS].T.astype(BF16)
            )
        return carry_value

    half = BLOCK_KEY_ROWS // 2
    for own_rows, fits in ((half, offset < half), (BLOCK_KEY_ROWS, offset >= half)):

        @pl.when(fits)
        def _(own_rows=own_rows):
            lax.fori_loop(0, GROUP_WIDTH // HEADS_STEP, functools.partial(step, own_rows), 0)

    @pl.when(t == last - 1)
    def _():
        if emit == "carry":
            copy = pltpu.make_async_copy(acc, outs[0], carry_sem)
            copy.start()
            copy.wait()
        elif emit == "joined":
            copies = []
            for column in range(lay.n_col):
                parts[column] = acc[column].astype(BF16)
                for row in range(lay.ny):
                    place_at = row * lay.n_col + column
                    copy = pltpu.make_async_copy(
                        parts.at[column], outs[0].at[place_at], part_sems.at[place_at]
                    )
                    copy.start()
                    copies.append(copy)
            for copy in copies:
                copy.wait()
        else:
            for s in range(lay.n_col):
                column = wrap(c + s, lay.n_col)
                outs[s][...] = acc[column, :, head:].astype(BF16)
                outs[lay.n_col + s][...] = acc[column, :, :head].astype(BF16)


def group_grads(lay, g, tiles, place, lists, queries, output_gradient, units, dq_in, carry, emit):
    first, last = tiles
    width = GROUP_WIDTH * HEAD_WIDTH
    wide = pl.BlockSpec((TILE_QUERY_ROWS, width), lambda t, *_: (t + first, g))
    keys_shape = (BLOCK_KEY_ROWS, HEAD_WIDTH)
    pair_shape = (BLOCK_KEY_ROWS, 2 * HEAD_WIDTH)
    acc_shape = (lay.n_col,) + pair_shape
    flat_units = list(units)
    extra = [x for x in (dq_in, carry) if x is not None]
    spec = (first, last, len(flat_units), int(dq_in is not None), carry is not None, emit)
    shapes = {
        "carry": [(acc_shape, F32)],
        "joined": [((lay.plane,) + pair_shape, BF16)],
        "split": [(keys_shape, BF16)] * (2 * lay.n_col),
    }[emit]
    flops = 10 * TILE_QUERY_ROWS * (last - first) * width * PICKED_BLOCKS * BLOCK_KEY_ROWS
    return pl.pallas_call(
        lambda *refs: grads_kernel(lay, spec, *refs),
        out_shape=[jax.ShapeDtypeStruct(queries.shape, BF16)]
        + [jax.ShapeDtypeStruct(*shape) for shape in shapes],
        grid_spec=pltpu.PrefetchScalarGridSpec(
            num_scalar_prefetch=2,
            grid=(last - first,),
            in_specs=[wide, wide] + hbm(len(flat_units) + len(extra)),
            out_specs=[wide]
            + (
                hbm(1)
                if emit != "split"
                else [pl.BlockSpec(s, lambda t, *_, n=len(s): (0,) * n) for s, _ in shapes]
            ),
            scratch_shapes=[
                pltpu.VMEM((lay.n_col,) + keys_shape, BF16),
                pltpu.VMEM((lay.n_col,) + keys_shape, BF16),
                pltpu.VMEM((lay.n_col, HEAD_WIDTH, BLOCK_KEY_ROWS), BF16),
                pltpu.VMEM(acc_shape, F32),
                pltpu.VMEM(acc_shape, BF16),
                pltpu.SemaphoreType.DMA((2, lay.plane)),
                pltpu.SemaphoreType.DMA,
                pltpu.SemaphoreType.DMA((lay.plane,)),
            ],
        ),
        input_output_aliases={} if dq_in is None else {4 + len(flat_units): 0},
        compiler_params=pltpu.CompilerParams(
            dimension_semantics=("arbitrary",), vmem_limit_bytes=VMEM_GRANT
        ),
        cost_estimate=pl.CostEstimate(
            flops=flops,
            bytes_accessed=6 * TILE_QUERY_ROWS * (last - first) * width,
            transcendentals=0,
        ),
    )(place, lists, queries, output_gradient, *flat_units, *extra)


def local(lay, queries, keys, values, output_gradient, tile_block_table):
    n_tiles = tile_block_table.shape[0]
    groups = keys.shape[1] // HEAD_WIDTH
    row, col = lax.axis_index("row"), lax.axis_index("col")
    me = row * lay.n_col + col
    devices = lay.n_row * lay.n_col
    start = devices * (keys.shape[0] - n_tiles * TILE_QUERY_ROWS)
    place = jnp.stack(
        [row >> lay.y_bits, row & (lay.ny - 1), col, me * n_tiles, jnp.int32(start)]
    ).astype(jnp.int32)

    def cut(array, g):
        return array[:, g * HEAD_WIDTH : (g + 1) * HEAD_WIDTH]

    def gather_z(unit):
        return [unit] + [lax.ppermute(unit, AXES, lay.along_z(k)) for k in range(1, lay.nz)]

    def spread(units):
        return [units[0]] + [
            lax.ppermute(units[j], AXES, lay.in_plane(j)) for j in range(1, lay.plane)
        ]

    def repeat(parts):
        return [parts[j % lay.n_col] for j in range(lay.plane)]

    def exchange(stack):
        return lax.all_to_all(
            stack, AXES, 0, 0, axis_index_groups=lay.plane_groups(), tiled=True
        )

    def finish(mine):
        return [mine[0]] + [lax.ppermute(mine[k], AXES, lay.along_z(k)) for k in range(1, lay.nz)]

    chunks = [[cut(keys, 0)], [cut(values, 0)]]
    chunks += [[cut(keys, g), cut(values, g)] for g in range(1, groups)]
    gathered = []
    for chunk in chunks:
        gathered.append(gather_z(jnp.concatenate(chunk, axis=1)))
    flat = tile_block_table.reshape(1, n_tiles * PICKED_BLOCKS)
    table = lax.all_gather(flat, "col", axis=0, tiled=True)
    tables = [table] + [
        lax.ppermute(table, AXES, lay.in_plane(jy * lay.n_col)) for jy in range(1, lay.ny)
    ]
    send, keep = make_plan(lay, place, tables)

    landed = []
    for n, units in enumerate(gathered):
        chosen = select_units(lay, place, send, units, n == 1)
        landed.append([exchange(chosen[0])] if n == 1 else spread(chosen))
    landed = [landed[0] + landed[1]] + landed[2:]
    fixed = (place, tile_block_table, queries, output_gradient)
    sums, waiting, dq = [], [], None
    for g in range(groups):
        emit = "joined" if g < groups - 1 else "split"
        dq, *parts = group_grads(
            lay, g, (0, n_tiles), *fixed, landed[g], dq, None, emit
        )
        if emit == "joined":
            waiting.append((((0, g), (1, g)), exchange(parts[0])))
    arrived, parts = lax.optimization_barrier(([units for _, units in waiting], parts))
    for (pieces, _), units in zip(waiting, arrived):
        sums.append((pieces, finish(combine_parts(lay, place, keep, units))))
    first = spread(repeat(parts[: lay.n_col]))
    second = spread(repeat(parts[lay.n_col :]))
    sums.append((((1, g),), finish(combine_parts(lay, place, keep, first))))
    sums.append((((0, g),), finish(combine_parts(lay, place, keep, second))))
    dkeys, dvalues = total_up(lay, sums, keys.shape)
    return dq, dkeys, dvalues


def solution(mesh):
    lay = Layout(mesh)
    spec = P(AXES, None)


    def body(*args):
        return local(lay, *args)

    return jax.shard_map(
        body, mesh=mesh, in_specs=(spec,) * 5, out_specs=(spec,) * 3, check_vma=False
    )
```

```python
import functools
import math

import jax
import jax.numpy as jnp
from jax import lax
from jax.experimental import pallas as pl
from jax.experimental.pallas import tpu as pltpu
from jax.sharding import PartitionSpec as P

HEAD_WIDTH = 128
GROUP_WIDTH = 16
TILE_QUERY_ROWS = 128
BLOCK_KEY_ROWS = 512
PICKED_BLOCKS = 3
HEADS_STEP = 8
SCALE = HEAD_WIDTH**-0.5
SCALE_LOG2 = SCALE * math.log2(math.e)
ROWS_ROWS = (((1,), (1,)), ((), ()))
VMEM_GRANT = 67043328
AXES = ("row", "col")

F32 = jnp.float32
BF16 = jnp.bfloat16


class Layout:
    def __init__(self, mesh):
        self.n_row = mesh.shape["row"]
        self.n_col = mesh.shape["col"]
        self.ny = 1
        while self.n_row % (2 * self.ny) == 0 and 4 * self.ny * self.ny <= self.n_row:
            self.ny *= 2
        self.nz = self.n_row // self.ny
        self.plane = self.ny * self.n_col
        self.col_bits = self.n_col.bit_length() - 1
        self.y_bits = self.ny.bit_length() - 1
        assert self.n_col == 1 << self.col_bits and self.n_row == self.nz << self.y_bits

    def col_of(self, block):
        return block & (self.n_col - 1)

    def y_of(self, block):
        return (block >> self.col_bits) & (self.ny - 1)

    def ahead(self, y, c, j):
        jy, jc = divmod(j, self.n_col)
        return wrap(y + jy, self.ny) * self.n_col + wrap(c + jc, self.n_col)

    def behind(self, y, c, j):
        jy, jc = divmod(j, self.n_col)
        return wrap(y - jy, self.ny) * self.n_col + wrap(c - jc, self.n_col)

    def plane_groups(self):
        return [
            [self.device(z, y, c) for y in range(self.ny) for c in range(self.n_col)]
            for z in range(self.nz)
        ]

    def z_of(self, block):
        return block >> (self.col_bits + self.y_bits)

    def device(self, z, y, c):
        return (z * self.ny + y) * self.n_col + c

    def everyone(self):
        return [
            (z, y, c) for z in range(self.nz) for y in range(self.ny) for c in range(self.n_col)
        ]

    def along_z(self, k):
        return [
            (self.device(z, y, c), self.device((z + k) % self.nz, y, c))
            for z, y, c in self.everyone()
        ]

    def in_plane(self, j):
        jy, jc = divmod(j, self.n_col)
        return [
            (self.device(z, y, c), self.device(z, (y + jy) % self.ny, (c + jc) % self.n_col))
            for z, y, c in self.everyone()
        ]


def wrap(value, size):
    return jnp.where(value >= size, value - size, jnp.where(value < 0, value + size, value))


def hbm(count):
    return [pl.BlockSpec(memory_space=pltpu.HBM)] * count


def smem(count):
    return [pl.BlockSpec(memory_space=pltpu.SMEM)] * count


def plan_kernel(lay, place, *refs):
    tables, (send, keep) = refs[: lay.ny], refs[lay.ny :]
    z, y, c = place[0], place[1], place[2]

    def wanted(table, device_col):
        block = jnp.int32(-1)
        for entry in range(table.shape[1]):
            named = table[device_col, entry]
            block = jnp.where((lay.col_of(named) == c) & (lay.y_of(named) == y), named, block)
        return block

    for j in range(lay.plane):
        jy, jc = divmod(j, lay.n_col)
        block = wanted(tables[(lay.ny - jy) % lay.ny], wrap(c + jc, lay.n_col))
        send[j] = jnp.where(block >= 0, wrap(z - lay.z_of(block), lay.nz), 0)
        block = wanted(tables[jy], wrap(c - jc, lay.n_col))
        keep[j] = jnp.where(block >= 0, wrap(lay.z_of(block) - z, lay.nz), -1)


def make_plan(lay, place, tables):
    count = jax.ShapeDtypeStruct((lay.plane,), jnp.int32)
    return pl.pallas_call(
        lambda *refs: plan_kernel(lay, *refs),
        out_shape=[count] * 2,
        in_specs=smem(1 + lay.ny),
        out_specs=smem(2),
        compiler_params=pltpu.CompilerParams(vmem_limit_bytes=VMEM_GRANT),
        name="make_plan",
    )(place, *tables)


def select_kernel(lay, joined, place, send, *refs):
    sources = refs[-3].shape[0]
    gathered, outs = refs[:sources], refs[sources:-3]
    held, in_sems, out_sems = refs[-3:]
    y, c = place[1], place[2]
    loads = [
        pltpu.make_async_copy(gathered[k], held.at[k], in_sems.at[k]) for k in range(sources)
    ]
    for load in loads:
        load.start()
    for load in loads:
        load.wait()
    stores = []
    for j in range(lay.plane):
        target = outs[0].at[lay.ahead(y, c, j)] if joined else outs[j]
        stores.append(pltpu.make_async_copy(held.at[send[j]], target, out_sems.at[j]))
    for store in stores:
        store.start()
    for store in stores:
        store.wait()


def select_units(lay, place, send, gathered, joined):
    unit = gathered[0]
    out = jax.ShapeDtypeStruct(((lay.plane,) if joined else ()) + unit.shape, unit.dtype)
    count = 1 if joined else lay.plane
    return pl.pallas_call(
        lambda *refs: select_kernel(lay, joined, *refs),
        out_shape=[out] * count,
        in_specs=smem(2) + hbm(len(gathered)),
        out_specs=hbm(count),
        scratch_shapes=[
            pltpu.VMEM((len(gathered),) + unit.shape, unit.dtype),
            pltpu.SemaphoreType.DMA((len(gathered),)),
            pltpu.SemaphoreType.DMA((lay.plane,)),
        ],
        compiler_params=pltpu.CompilerParams(vmem_limit_bytes=VMEM_GRANT),
        name="select_units",
    )(place, send, *gathered)


def combine_kernel(lay, n_parts, place, keep, *refs):
    parts, outs = refs[:n_parts], refs[n_parts : n_parts + lay.nz]
    held, acc, sems = refs[n_parts + lay.nz :]
    y, c = place[1], place[2]
    loads = []
    for j in range(lay.plane):
        source = parts[0].at[lay.behind(y, c, j)] if n_parts == 1 else parts[j]
        loads.append(pltpu.make_async_copy(source, held.at[j], sems.at[j]))
    for j in range(lay.plane):

        @pl.when(keep[j] >= 0)
        def _(j=j):
            loads[j].start()

    acc[...] = jnp.zeros_like(acc)
    for j in range(lay.plane):

        @pl.when(keep[j] >= 0)
        def _(j=j):
            loads[j].wait()
            acc[keep[j]] += held[j].astype(F32)

    for k in range(lay.nz):
        outs[k][...] = acc[k].astype(BF16)


def combine_parts(lay, place, keep, parts):
    joined = not isinstance(parts, list)
    parts = [parts] if joined else parts
    unit = jax.ShapeDtypeStruct(parts[0].shape[-2:], parts[0].dtype)
    return pl.pallas_call(
        lambda *refs: combine_kernel(lay, len(parts), *refs),
        out_shape=[jax.ShapeDtypeStruct(unit.shape, unit.dtype)] * lay.nz,
        in_specs=smem(2) + hbm(len(parts)),
        out_specs=[pl.BlockSpec(memory_space=pltpu.VMEM)] * lay.nz,
        scratch_shapes=[
            pltpu.VMEM((lay.plane,) + unit.shape, unit.dtype),
            pltpu.VMEM((lay.nz,) + unit.shape, F32),
            pltpu.SemaphoreType.DMA((lay.plane,)),
        ],
        compiler_params=pltpu.CompilerParams(vmem_limit_bytes=VMEM_GRANT),
        name="combine_parts",
    )(place, keep, *parts)


def added(lay, terms):
    total = terms[0][...].astype(F32)
    for term in terms[1 : lay.nz]:
        total += term[...].astype(F32)
    return total.astype(BF16)


def total_kernel(lay, widths, *refs):
    terms, (dkeys, dvalues) = refs[:-2], refs[-2:]
    for n, pieces in enumerate(widths):
        total = added(lay, terms[n * lay.nz :])
        for piece, (which, g) in enumerate(pieces):
            out = (dkeys, dvalues)[which]
            out[:, g * HEAD_WIDTH : (g + 1) * HEAD_WIDTH] = total[
                :, piece * HEAD_WIDTH : (piece + 1) * HEAD_WIDTH
            ]


def total_up(lay, sums, shape):
    terms = [term for _, received in sums for term in received]
    return pl.pallas_call(
        lambda *refs: total_kernel(lay, [pieces for pieces, _ in sums], *refs),
        out_shape=[jax.ShapeDtypeStruct(shape, BF16)] * 2,
        in_specs=[pl.BlockSpec(memory_space=pltpu.VMEM)] * len(terms),
        out_specs=[pl.BlockSpec(memory_space=pltpu.VMEM)] * 2,
        compiler_params=pltpu.CompilerParams(vmem_limit_bytes=VMEM_GRANT),
        name="total_up",
    )(*terms)


def last_kernel(lay, *refs):
    refs[-1][...] = added(lay, refs[: lay.nz])


def total_last(lay, terms, g, dkeys):
    unit = pl.BlockSpec(terms[0].shape, lambda i: (0, 0))
    return pl.pallas_call(
        lambda *refs: last_kernel(lay, *refs),
        out_shape=jax.ShapeDtypeStruct(dkeys.shape, dkeys.dtype),
        grid=(1,),
        in_specs=[unit] * lay.nz + hbm(1),
        out_specs=pl.BlockSpec(terms[0].shape, lambda i: (0, g)),
        input_output_aliases={lay.nz: 0},
        compiler_params=pltpu.CompilerParams(vmem_limit_bytes=VMEM_GRANT),
        name="total_last",
    )(*terms, dkeys)


def grads_kernel(lay, spec, place, lists, q, do, *refs):
    first, last, n_units, has_dq, has_carry, emit = spec
    units, refs = refs[:n_units], refs[n_units + has_dq :]
    carry, refs = (refs[0], refs[1:]) if has_carry else (None, refs)
    n_out = {"carry": 1, "joined": 1, "split": 2 * lay.n_col}[emit]
    dq, outs, refs = refs[0], refs[1 : 1 + n_out], refs[1 + n_out :]
    k_rows, v_rows, kt, acc, parts, sems, carry_sem, part_sems = refs
    y, c, tile0, start = place[1], place[2], place[3], place[4]
    t = pl.program_id(0) + first
    head = HEAD_WIDTH
    rows = HEADS_STEP * TILE_QUERY_ROWS

    @pl.when(t == first)
    def _():
        if has_carry:
            carried = pltpu.make_async_copy(carry, acc, carry_sem)
            carried.start()
        copies = []
        for column in range(lay.n_col):
            block = jnp.int32(-1)
            for tile in range(first, last):
                for pick in range(PICKED_BLOCKS):
                    named = lists[tile, pick]
                    block = jnp.where(lay.col_of(named) == column, named, block)
            from_y = lay.y_of(block)
            hops = wrap(y - from_y, lay.ny) * lay.n_col + wrap(c - column, lay.n_col)
            pairs = []
            for j in range(lay.plane):
                needed = (block >= 0) & (hops == j)
                if n_units == lay.plane:
                    pairs.append((needed, 0, units[j].at[:, :head], k_rows))
                    pairs.append((needed, 1, units[j].at[:, head:], v_rows))
                else:
                    pairs.append((needed, 0, units[j], k_rows))
            if n_units > lay.plane:
                here = units[lay.plane].at[from_y * lay.n_col + column]
                pairs.append((block >= 0, 1, here, v_rows))
            for needed, n, source, target in pairs:
                copy = pltpu.make_async_copy(source, target.at[column], sems.at[n, column])
                copies.append((needed, copy))
        for needed, copy in copies:
            pl.when(needed)(copy.start)
        if not has_carry:
            acc[...] = jnp.zeros_like(acc)
        for needed, copy in copies:
            pl.when(needed)(copy.wait)
        for column in range(lay.n_col):
            kt[column] = k_rows[column].T
        if has_carry:
            carried.wait()

    slots = [lay.col_of(lists[t, pick]) for pick in range(PICKED_BLOCKS)]
    offset = start + (tile0 + t) * TILE_QUERY_ROWS - lists[t, 0] * BLOCK_KEY_ROWS

    def step(own_rows, i, carry_value):
        base = pl.multiple_of(i * rows, rows)
        q_rows = jnp.concatenate([q[:, pl.ds(base + h * head, head)] for h in range(HEADS_STEP)], 0)
        do_rows = jnp.concatenate(
            [do[:, pl.ds(base + h * head, head)] for h in range(HEADS_STEP)], 0
        )
        seen = [own_rows] + [BLOCK_KEY_ROWS] * (PICKED_BLOCKS - 1)
        scores = [
            lax.dot_general(k_rows[s, :n], q_rows, ROWS_ROWS, preferred_element_type=F32)
            for s, n in zip(slots, seen)
        ]
        key_at = lax.broadcasted_iota(jnp.int32, (own_rows, rows), 0)
        query_at = lax.broadcasted_iota(jnp.int32, (own_rows, rows), 1)
        query_at = (query_at & (TILE_QUERY_ROWS - 1)) + offset
        scores[0] = jnp.where(key_at <= query_at, scores[0], -jnp.inf)
        top = jnp.max(scores[0], axis=0, keepdims=True)
        for s in scores[1:]:
            top = jnp.maximum(top, jnp.max(s, axis=0, keepdims=True))
        top = top * SCALE_LOG2
        exps = [jnp.exp2(s * SCALE_LOG2 - top) for s in scores]
        gw = [
            lax.dot_general(v_rows[s, :n], do_rows, ROWS_ROWS, preferred_element_type=F32)
            for s, n in zip(slots, seen)
        ]
        inverse = 1.0 / sum(jnp.sum(e, axis=0, keepdims=True) for e in exps)
        delta = inverse * sum(jnp.sum(e * g, axis=0, keepdims=True) for e, g in zip(exps, gw))
        dq_t = jnp.zeros((head, rows), F32)
        for s, n, e, g in zip(slots, seen, exps, gw):
            weights = e * inverse
            gs = (weights * ((g - delta) * SCALE)).astype(BF16)
            acc[s, :n, :head] += jnp.dot(gs, q_rows, preferred_element_type=F32)
            acc[s, :n, head:] += jnp.dot(
                weights.astype(BF16), do_rows, preferred_element_type=F32
            )
            dq_t += jnp.dot(kt[s, :, :n], gs, preferred_element_type=F32)
        for h in range(HEADS_STEP):
            dq[:, pl.ds(base + h * head, head)] = (
                dq_t[:, h * TILE_QUERY_ROWS : (h + 1) * TILE_QUERY_ROWS].T.astype(BF16)
            )
        return carry_value

    half = BLOCK_KEY_ROWS // 2
    for own_rows, fits in ((half, offset < half), (BLOCK_KEY_ROWS, offset >= half)):

        @pl.when(fits)
        def _(own_rows=own_rows):
            lax.fori_loop(0, GROUP_WIDTH // HEADS_STEP, functools.partial(step, own_rows), 0)

    @pl.when(t == last - 1)
    def _():
        if emit == "carry":
            copy = pltpu.make_async_copy(acc, outs[0], carry_sem)
            copy.start()
            copy.wait()
        elif emit == "joined":
            copies = []
            for column in range(lay.n_col):
                parts[column] = acc[column].astype(BF16)
                for row in range(lay.ny):
                    place_at = row * lay.n_col + column
                    copy = pltpu.make_async_copy(
                        parts.at[column], outs[0].at[place_at], part_sems.at[place_at]
                    )
                    copy.start()
                    copies.append(copy)
            for copy in copies:
                copy.wait()
        else:
            for s in range(lay.n_col):
                column = wrap(c + s, lay.n_col)
                outs[s][...] = acc[column, :, head:].astype(BF16)
                outs[lay.n_col + s][...] = acc[column, :, :head].astype(BF16)


def group_grads(lay, g, tiles, place, lists, queries, output_gradient, units, dq_in, carry, emit):
    first, last = tiles
    width = GROUP_WIDTH * HEAD_WIDTH
    wide = pl.BlockSpec((TILE_QUERY_ROWS, width), lambda t, *_: (t + first, g))
    keys_shape = (BLOCK_KEY_ROWS, HEAD_WIDTH)
    pair_shape = (BLOCK_KEY_ROWS, 2 * HEAD_WIDTH)
    acc_shape = (lay.n_col,) + pair_shape
    flat_units = list(units)
    extra = [x for x in (dq_in, carry) if x is not None]
    spec = (first, last, len(flat_units), int(dq_in is not None), carry is not None, emit)
    shapes = {
        "carry": [(acc_shape, F32)],
        "joined": [((lay.plane,) + pair_shape, BF16)],
        "split": [(keys_shape, BF16)] * (2 * lay.n_col),
    }[emit]
    flops = 10 * TILE_QUERY_ROWS * (last - first) * width * PICKED_BLOCKS * BLOCK_KEY_ROWS
    return pl.pallas_call(
        lambda *refs: grads_kernel(lay, spec, *refs),
        out_shape=[jax.ShapeDtypeStruct(queries.shape, BF16)]
        + [jax.ShapeDtypeStruct(*shape) for shape in shapes],
        grid_spec=pltpu.PrefetchScalarGridSpec(
            num_scalar_prefetch=2,
            grid=(last - first,),
            in_specs=[wide, wide] + hbm(len(flat_units) + len(extra)),
            out_specs=[wide]
            + (
                hbm(1)
                if emit != "split"
                else [pl.BlockSpec(s, lambda t, *_, n=len(s): (0,) * n) for s, _ in shapes]
            ),
            scratch_shapes=[
                pltpu.VMEM((lay.n_col,) + keys_shape, BF16),
                pltpu.VMEM((lay.n_col,) + keys_shape, BF16),
                pltpu.VMEM((lay.n_col, HEAD_WIDTH, BLOCK_KEY_ROWS), BF16),
                pltpu.VMEM(acc_shape, F32),
                pltpu.VMEM(acc_shape, BF16),
                pltpu.SemaphoreType.DMA((2, lay.plane)),
                pltpu.SemaphoreType.DMA,
                pltpu.SemaphoreType.DMA((lay.plane,)),
            ],
        ),
        input_output_aliases={} if dq_in is None else {4 + len(flat_units): 0},
        compiler_params=pltpu.CompilerParams(
            dimension_semantics=("arbitrary",), vmem_limit_bytes=VMEM_GRANT
        ),
        cost_estimate=pl.CostEstimate(
            flops=flops,
            bytes_accessed=6 * TILE_QUERY_ROWS * (last - first) * width,
            transcendentals=0,
        ),
    )(place, lists, queries, output_gradient, *flat_units, *extra)


def local(lay, queries, keys, values, output_gradient, tile_block_table):
    n_tiles = tile_block_table.shape[0]
    groups = keys.shape[1] // HEAD_WIDTH
    row, col = lax.axis_index("row"), lax.axis_index("col")
    me = row * lay.n_col + col
    devices = lay.n_row * lay.n_col
    start = devices * (keys.shape[0] - n_tiles * TILE_QUERY_ROWS)
    place = jnp.stack(
        [row >> lay.y_bits, row & (lay.ny - 1), col, me * n_tiles, jnp.int32(start)]
    ).astype(jnp.int32)

    def cut(array, g):
        return array[:, g * HEAD_WIDTH : (g + 1) * HEAD_WIDTH]

    def gather_z(unit):
        return [unit] + [lax.ppermute(unit, AXES, lay.along_z(k)) for k in range(1, lay.nz)]

    def spread(units):
        return [units[0]] + [
            lax.ppermute(units[j], AXES, lay.in_plane(j)) for j in range(1, lay.plane)
        ]

    def repeat(parts):
        return [parts[j % lay.n_col] for j in range(lay.plane)]

    def exchange(stack):
        return lax.all_to_all(
            stack, AXES, 0, 0, axis_index_groups=lay.plane_groups(), tiled=True
        )

    def finish(mine):
        return [mine[0]] + [lax.ppermute(mine[k], AXES, lay.along_z(k)) for k in range(1, lay.nz)]

    chunks = [[cut(keys, 0)], [cut(values, 0)]]
    chunks += [[cut(keys, g), cut(values, g)] for g in range(1, groups)]
    gathered = []
    for chunk in chunks:
        gathered.append(gather_z(jnp.concatenate(chunk, axis=1)))
    flat = tile_block_table.reshape(1, n_tiles * PICKED_BLOCKS)
    table = lax.all_gather(flat, "col", axis=0, tiled=True)
    tables = [table] + [
        lax.ppermute(table, AXES, lay.in_plane(jy * lay.n_col)) for jy in range(1, lay.ny)
    ]
    send, keep = make_plan(lay, place, tables)

    landed = []
    for n, units in enumerate(gathered):
        chosen = select_units(lay, place, send, units, n == 1)
        landed.append([exchange(chosen[0])] if n == 1 else spread(chosen))
    landed = [landed[0] + landed[1]] + landed[2:]
    fixed = (place, tile_block_table, queries, output_gradient)
    sums, waiting, dq = [], [], None
    for g in range(groups):
        emit = "joined" if g < groups - 1 else "split"
        dq, *parts = group_grads(
            lay, g, (0, n_tiles), *fixed, landed[g], dq, None, emit
        )
        if emit == "joined":
            waiting.append((((0, g), (1, g)), exchange(parts[0])))
    arrived, parts = lax.optimization_barrier(([units for _, units in waiting], parts))
    for (pieces, _), units in zip(waiting, arrived):
        sums.append((pieces, finish(combine_parts(lay, place, keep, units))))
    first = spread(repeat(parts[: lay.n_col]))
    second = spread(repeat(parts[lay.n_col :]))
    sums.append((((1, g),), finish(combine_parts(lay, place, keep, first))))
    sums.append((((0, g),), finish(combine_parts(lay, place, keep, second))))
    dkeys, dvalues = total_up(lay, sums[:-1], keys.shape)
    dkeys = total_last(lay, sums[-1][1], groups - 1, dkeys)
    return dq, dkeys, dvalues


def solution(mesh):
    spec = P(AXES, None)


    def body(*args):
        lay = Layout(mesh)
        return local(lay, *args)

    return jax.shard_map(
        body, mesh=mesh, in_specs=(spec,) * 5, out_specs=(spec,) * 3, check_vma=False
    )
```
